256 devices in a mesh: slab: 64 (over y, x_hi, z), sub: 4 (over x_lo, core).
Axes of the slice: x: 4 (x_hi: 2, x_lo: 2; x = x_hi * 2 + x_lo), y: 4, z: 8, core: 2. Of those that a mesh axis runs over, the one named last changes fastest.
Arguments:
- right_sides: bfloat16 [524288, 768], P(('slab', 'sub')), may hold values from -6 to 6
- front_sides: bfloat16 [131072, 768], P(('slab', 'sub')), may hold values from -6 to 6
- pending_front: bfloat16 [131072, 256], P(('slab', 'sub')), may hold values from -6 to 6
- inner_index: int32 [4096, 6], P(('slab', 'sub')), may hold values from 0 to 15, all different within a row
- inner_blocks: bfloat16 [4096, 6, 128, 128], P(('slab', 'sub')), may hold values from -0.15625 to 0.15625
- inner_inverse: bfloat16 [4096, 128, 128], P(('slab', 'sub')), may hold values from -1 to 2
- outer_index: int32 [1024, 8], P(('slab', 'sub')), may hold values from 0 to 15, all different within a row
- outer_blocks: bfloat16 [1024, 8, 128, 128], P(('slab', 'sub')), may hold values from -0.125 to 0.125
- front_inverse: bfloat16 [1024, 128, 128], P(('slab', 'sub')), may hold values from -1 to 2
Outputs:
- solution: bfloat16 [524288, 768], P(('slab', 'sub'))
- front_solution: bfloat16 [131072, 768], P(('slab', 'sub'))
The draws below stay inside these ranges and needn't reach their ends.
All inputs are finite; a program needn't handle non-finite values.
Results may differ from the reference program's by a relative error of at most 0.009.
Values may be sent and summed in bfloat16 or wider, within the bound.
A program may use at most 64 MiB of HBM per device.

```python
import math
import jax
import jax.numpy as jnp
from jax import lax

BLOCK = 128
FRONT = 2048
COLUMNS = 256
TICKS = 3
ROWS_DEV = 2048
FRONT_LINKS = 6
INNER_LINKS = 8
ROWS = 524288
FRONTS = 131072
N_SLAB = 64
N_SUB = 4


def block_inverse(key, block_count):
    random_part = jax.random.truncated_normal(key, -4.0, 4.0, (block_count, BLOCK, BLOCK), jnp.float32)
    matrix = jnp.eye(BLOCK, dtype=jnp.float32)[None] + 0.5 * random_part / math.sqrt(BLOCK)
    return matrix.astype(jnp.bfloat16)


def draw_inner_inverse(key, part):
    return block_inverse(jax.random.fold_in(key, 11), ROWS // BLOCK)


def draw_front_inverse(key, part):
    return block_inverse(jax.random.fold_in(key, 23), FRONTS // BLOCK)


def levels(own_key, extent, split, smallest, top_value):
    def one(axis_at, parts):
        draws = jax.random.uniform(jax.random.fold_in(jax.random.fold_in(own_key, 6), axis_at), (parts,), jnp.float32, smallest / len(split), top_value / len(split))
        return jnp.repeat(jnp.exp(draws), extent[axis_at] // parts).reshape((-1,) + (1,) * (len(extent) - axis_at - 1))

    loudness = one(*split[0])
    for cut in split[1:]:
        loudness = loudness * one(*cut)
    return loudness


def picks_of(stream_key, rows, count, top, lift):
    sequence = jax.random.permutation(jax.random.fold_in(stream_key, 1), count)
    favour = sequence
    for power in range(3):
        favour = favour * favour // count
    favour = favour * lift // count
    tickets = jax.random.randint(jax.random.fold_in(stream_key, 2), (rows, count), 0, 4096) + favour
    sure = jax.random.permutation(jax.random.fold_in(stream_key, 3), rows)[jnp.arange(count) % rows]
    tickets = jnp.where(jnp.arange(rows)[:, None] == sure[None, :], 1 << 14, tickets)
    merit = tickets * count + jnp.arange(count)
    return lax.top_k(merit.astype(jnp.int32), top)[1].astype(jnp.int32)


def normal_values(key, shape, width, reach, pieces=(), kind=jnp.bfloat16):
    factor_of = levels(key, shape, pieces, -0.22, 0.18) if pieces else 1.0
    array = jax.random.normal(key, shape, jnp.float32) * width * factor_of
    return jnp.minimum(jnp.maximum(array, -reach), reach).astype(kind)


def setup_inputs(seed: int = 0) -> dict:
    key_of = jax.random.split(jax.random.key(seed), 10)
    return {
        "right_sides": normal_values(key_of[0], (ROWS, TICKS * COLUMNS), 1.0, 6.0, ((0, 256),)),
        "front_sides": normal_values(key_of[1], (FRONTS, TICKS * COLUMNS), 1.0, 6.0, ((0, 256),)),
        "pending_front": normal_values(key_of[2], (FRONTS, COLUMNS), 1.0, 6.0, ((0, 256),)),
        "inner_index": picks_of(key_of[3], (ROWS // BLOCK), FRONT // BLOCK, FRONT_LINKS, 0),
        "inner_blocks": normal_values(key_of[4], (ROWS // BLOCK, FRONT_LINKS, BLOCK, BLOCK), (2 * FRONT_LINKS * BLOCK) ** -0.5, 0.15625, ((0, 256),)),
        "inner_inverse": draw_inner_inverse(jax.random.fold_in(key_of[9], 71), 0),
        "outer_index": picks_of(key_of[6], (FRONTS // BLOCK), ROWS_DEV // BLOCK, INNER_LINKS, 0),
        "outer_blocks": normal_values(key_of[7], (FRONTS // BLOCK, INNER_LINKS, BLOCK, BLOCK), (2 * INNER_LINKS * BLOCK) ** -0.5, 0.125, ((0, 256),)),
        "front_inverse": draw_front_inverse(jax.random.fold_in(key_of[9], 71), 0),
    }


def slab_group(operands):
    inner_sides, outer_sides, arriving, in_index, in_blocks, in_inverse, out_index, out_blocks, out_inverse = operands
    front_blocks = arriving.reshape(FRONT // BLOCK, BLOCK, COLUMNS)
    picked = front_blocks[in_index]
    coupled = jnp.einsum("qikab,qikbc->qiac", in_blocks.astype(jnp.float32), picked.astype(jnp.float32))
    inner_values = lax.optimization_barrier((inner_sides.astype(jnp.float32) - coupled).astype(jnp.bfloat16))
    solved = jnp.einsum("qiab,qibc->qiac", in_inverse.astype(jnp.float32), inner_values.astype(jnp.float32))
    solved = lax.optimization_barrier(solved.astype(jnp.bfloat16))
    chosen = jax.vmap(lambda values, where: values[where])(solved, out_index)
    outgoing = jnp.einsum("qjkab,qjkbc->qjac", out_blocks.astype(jnp.float32), chosen.astype(jnp.float32))
    outer_values = lax.optimization_barrier((outer_sides.astype(jnp.float32) - outgoing).astype(jnp.bfloat16))
    front_done = jnp.einsum("qjab,qjbc->qjac", out_inverse.astype(jnp.float32), outer_values.astype(jnp.float32))
    return solved, front_done.astype(jnp.bfloat16)


def reference(right_sides, front_sides, pending_front, inner_index, inner_blocks, inner_inverse, outer_index, outer_blocks, front_inverse):
    slabs = N_SLAB
    subs = N_SUB
    inner_rows = ROWS_DEV // BLOCK
    outer_rows = FRONT // (subs * BLOCK)
    sides_all = right_sides.reshape(slabs, subs, inner_rows, BLOCK, TICKS, COLUMNS)
    front_all = front_sides.reshape(slabs, subs, outer_rows, BLOCK, TICKS, COLUMNS)
    in_index = inner_index.reshape(slabs, subs, inner_rows, FRONT_LINKS)
    in_blocks = inner_blocks.reshape(slabs, subs, inner_rows, FRONT_LINKS, BLOCK, BLOCK)
    in_inverse = inner_inverse.reshape(slabs, subs, inner_rows, BLOCK, BLOCK)
    out_index = outer_index.reshape(slabs, subs, outer_rows, INNER_LINKS)
    out_blocks = outer_blocks.reshape(slabs, subs, outer_rows, INNER_LINKS, BLOCK, BLOCK)
    out_inverse = front_inverse.reshape(slabs, subs, outer_rows, BLOCK, BLOCK)
    arriving = pending_front.reshape(slabs, FRONT, COLUMNS)
    solved_list = []
    front_list = []
    for group in range(TICKS):
        solved, front_done = lax.map(slab_group, (sides_all[:, :, :, :, group, :], front_all[:, :, :, :, group, :], arriving, in_index, in_blocks, in_inverse, out_index, out_blocks, out_inverse))
        solved_list.append(solved)
        front_list.append(front_done)
        whole = front_done.reshape(slabs, FRONT, COLUMNS)
        arriving = jnp.concatenate([jnp.zeros((1, FRONT, COLUMNS), jnp.bfloat16), whole[:-1]], axis=0)
    solution = jnp.stack(solved_list, axis=4).reshape(ROWS, TICKS * COLUMNS)
    front_solution = jnp.stack(front_list, axis=4).reshape(FRONTS, TICKS * COLUMNS)
    return solution, front_solution
```

```python
import jax
import jax.numpy as jnp
from jax import lax
from jax.experimental import pallas as pl
from jax.experimental.pallas import tpu as pltpu
from jax.sharding import PartitionSpec as P

BF = jnp.bfloat16
F32 = jnp.float32
MESH = pl.DeviceIdType.MESH
BL = 128
NI = 16
NL = 6
NJ = 4
NK = 8
NF = 16
NT = 3
CW = 256
HW = 128


def lanes(parts):
    return jnp.concatenate(parts, axis=1)


def rows(parts):
    return jnp.concatenate(parts, axis=0)


def mm(a, b):
    return jnp.dot(a, b, preferred_element_type=F32)


def kernel(
    n_slab,
    iidx,
    oidx,
    rhs_h,
    front_h,
    pend_h,
    a_h,
    inv_h,
    b_h,
    finv_h,
    sol_h,
    fro_h,
    f00,
    f01,
    f10,
    f11,
    f20,
    f21,
    a,
    inv,
    b,
    finv,
    rhs,
    front,
    p32,
    pbf,
    cmat,
    w,
    y,
    ysend,
    s,
    pos,
    load_sem,
    out_sem,
    send_z,
    recv_z,
    send_s,
    recv_s,
    send_x,
    recv_x,
    send_xs,
    recv_xs,
):
    fr = ((f00, f01), (f10, f11), (f20, f21))
    slab = lax.axis_index("slab")
    sub = lax.axis_index("sub")
    sib = sub + 1 - 2 * (sub % 2)
    xp = (sub + 2) % 4
    crossed_out = ((slab + 1) % 8 == 0).astype(jnp.int32)
    crossed_in = (slab % 8 == 0).astype(jnp.int32)
    nxt = (slab + 1) % n_slab
    prv = (slab + n_slab - 1) % n_slab
    to_sub = (sub + 2 * crossed_out) % 4
    from_sub = (sub + 2 * crossed_in) % 4
    last = slab == n_slab - 1

    sib_id = (slab, sib)
    x_id = (slab, xp)
    next_id = (nxt, to_sub)
    prev_id = (prv, from_sub)

    barrier = pltpu.get_barrier_semaphore()
    for peer in (sib_id, x_id, next_id, prev_id):
        pl.semaphore_signal(barrier, inc=1, device_id=peer, device_id_type=MESH)

    def share(t):
        base = sub if t == 0 else from_sub
        one = base + 1 - 2 * (base % 2)
        return (base, one, (base + 2) % 4, (one + 2) % 4)

    loads = []

    def load(src, dst):
        copy = pltpu.make_async_copy(src, dst, load_sem.at[len(loads)])
        copy.start()
        loads.append(copy)
        return copy

    own = [
        [
            load(
                pend_h.at[:, :, c * HW : (c + 1) * HW],
                fr[0][c].at[pl.ds(4 * sub, 4)],
            )
            for c in range(1)
        ]
    ][0]
    ld_inv = load(inv_h, inv)
    ld_a = [
        load(a_h.at[pl.ds(4 * g, 4)], a.at[pl.ds(4 * g, 4), pl.ds(0, NL)])
        for g in range(4)
    ]
    ld_finv = load(finv_h, finv)
    ld_b = load(b_h, b)
    own.append(load(pend_h.at[:, :, HW:CW], fr[0][1].at[pl.ds(4 * sub, 4)]))
    ld_r = [load(rhs_h.at[:, :, 0:CW], rhs.at[0])]
    ld_g = load(front_h, front)
    for t in range(1, NT):
        ld_r.append(load(rhs_h.at[:, :, t * CW : (t + 1) * CW], rhs.at[t]))

    sends = []

    def send(src, dst, ssem, rsem, peer):
        copy = pltpu.make_async_remote_copy(
            src_ref=src,
            dst_ref=dst,
            send_sem=ssem,
            recv_sem=rsem,
            device_id=peer,
            device_id_type=MESH,
        )
        copy.start()
        sends.append(copy)

    def arrival(t, c, which, p, rsem):
        block = fr[t][c].at[4 * share(t)[which] + p]
        return pltpu.make_async_copy(block, block, rsem.at[t, c, p])

    pl.semaphore_wait(barrier, 4)

    base0 = share(0)[0]
    for c in range(2):
        for p in range(NJ):
            src = pend_h.at[p, :, c * HW : (c + 1) * HW]
            dst = fr[0][c].at[4 * base0 + p]
            send(src, dst, send_x.at[0, c, p], recv_x.at[0, c, p], x_id)
            send(src, dst, send_s.at[0, c, p], recv_s.at[0, c, p], sib_id)

    def fwd_z(t, c, p):
        arrival(t, c, 0, p, recv_z).wait()
        block = fr[t][c].at[4 * share(t)[0] + p]
        send(block, block, send_x.at[t, c, p], recv_x.at[t, c, p], x_id)
        send(block, block, send_s.at[t, c, p], recv_s.at[t, c, p], sib_id)

    def fwd_x(t, c, p):
        arrival(t, c, 2, p, recv_x).wait()
        block = fr[t][c].at[4 * share(t)[2] + p]
        send(block, block, send_xs.at[t, c, p], recv_xs.at[t, c, p], sib_id)

    def place(i, carry):
        own_links = [iidx[i, k] for k in range(NL)]
        for f in range(NF):
            at = jnp.int32(NL)
            for k in range(NL):
                at = jnp.where(own_links[k] == f, jnp.int32(k), at)
            pos[i * NF + f] = at
        return carry

    lax.fori_loop(0, NI, place, 0)

    for i in range(NI):
        a[i, NL] = jnp.zeros((BL, BL), BF)

    ld_inv.wait()
    for g in range(4):
        ld_a[g].wait()
        for i in range(4 * g, 4 * g + 4):
            for m in range(0, NL, 2):
                o = mm(inv[i], lanes([a[i, m], a[i, m + 1]]))
                o = (-o).astype(BF)
                a[i, m] = o[:, :BL]
                a[i, m + 1] = o[:, BL:]

    ld_finv.wait()
    ld_b.wait()
    for j in range(NJ):
        for m in range(0, NK, 2):
            o = mm(finv[j], lanes([b[j, m], b[j, m + 1]]))
            o = (-o).astype(BF)
            b[j, m] = o[:, :BL]
            b[j, m + 1] = o[:, BL:]

    def c_step(g):
        for j in range(NJ):
            tiles = []
            for k in range(NK):
                at = oidx[j, k]
                tiles.append(
                    lanes(
                        [
                            a[at, pos[at * NF + 2 * g]],
                            a[at, pos[at * NF + 2 * g + 1]],
                        ]
                    )
                )
            o = mm(lanes([b[j, k] for k in range(NK)]), rows(tiles)).astype(BF)
            cmat[2 * g, pl.ds(j * BL, BL)] = o[:, :BL]
            cmat[2 * g + 1, pl.ds(j * BL, BL)] = o[:, BL:]

    for g in range(NF // 2):
        c_step(g)
        if g in (2, 4, 6):
            fwd_x(0, 0, g // 2 - 1)

    def p_step(t):
        ld_r[t].wait()
        for i in range(NI):
            o = mm(inv[i], rhs[t, i])
            p32[t, i] = o
            pbf[t, i] = o.astype(BF)

    def w_step(t):
        if t == 0:
            ld_g.wait()
        for j in range(NJ):
            left = lanes([finv[j]] + [b[j, k] for k in range(NK)])
            right = rows(
                [front[j, :, t * CW : (t + 1) * CW]]
                + [pbf[t, oidx[j, k]] for k in range(NK)]
            )
            o = mm(left, right)
            w[t, 0, pl.ds(j * BL, BL)] = o[:, :HW]
            w[t, 1, pl.ds(j * BL, BL)] = o[:, HW:]

    def acc(t, c, which):
        sh = share(t)[which]
        if which == 0 and t == 0:
            own[c].wait()
        elif which == 1:
            for p in range(NJ):
                arrival(t, c, 1, p, recv_s).wait()
        elif which == 3:
            for p in range(NJ):
                arrival(t, c, 3, p, recv_xs).wait()
        left = lanes([cmat[4 * sh + r] for r in range(4)])
        right = fr[t][c][pl.ds(4 * sh, 4)].reshape(4 * BL, HW)
        w[t, c] = w[t, c] + mm(left, right)

    outs = []

    def put(src, dst):
        copy = pltpu.make_async_copy(src, dst, out_sem.at[len(outs)])
        copy.start()
        outs.append(copy)

    def y_step(t, c):
        value = w[t, c].astype(BF)
        if t + 1 < NT:
            passed = jnp.where(last, jnp.zeros_like(value), value)
            ysend[t, c] = passed.reshape(NJ, BL, HW)
            for p in range(NJ):
                send(
                    ysend.at[t, c, p],
                    fr[t + 1][c].at[4 * sub + p],
                    send_z.at[t + 1, c, p],
                    recv_z.at[t + 1, c, p],
                    next_id,
                )
        y[t, c] = value.reshape(NJ, BL, HW)
        at = t * CW + c * HW
        put(y.at[t, c], fro_h.at[:, :, at : at + HW])

    def s_step(t, g):
        for i in range(4 * g, 4 * g + 4):
            left = lanes([a[i, k] for k in range(NL)])
            right = rows(
                [
                    lanes([fr[t][0][iidx[i, k]], fr[t][1][iidx[i, k]]])
                    for k in range(NL)
                ]
            )
            s[t, i] = (p32[t, i] + mm(left, right)).astype(BF)
        put(
            s.at[t, pl.ds(4 * g, 4)],
            sol_h.at[pl.ds(4 * g, 4), :, t * CW : (t + 1) * CW],
        )

    p_step(0)
    fwd_x(0, 0, 3)
    w_step(0)
    fwd_x(0, 1, 0)
    for which in range(4):
        acc(0, 0, which)
    y_step(0, 0)
    fwd_x(0, 1, 1)
    p_step(1)
    fwd_x(0, 1, 2)
    acc(0, 1, 0)
    acc(0, 1, 1)
    fwd_x(0, 1, 3)
    w_step(1)
    acc(0, 1, 2)
    acc(0, 1, 3)
    y_step(0, 1)

    for t in range(NT - 1):
        n = t + 1
        for p in range(NJ):
            fwd_z(n, 0, p)
            s_step(t, p)
        if n + 1 < NT:
            p_step(n + 1)
            fwd_x(n, 0, 0)
            fwd_z(n, 1, 0)
            w_step(n + 1)
        else:
            fwd_x(n, 0, 0)
            fwd_z(n, 1, 0)
        acc(n, 0, 0)
        fwd_x(n, 0, 1)
        fwd_z(n, 1, 1)
        acc(n, 0, 1)
        fwd_x(n, 0, 2)
        fwd_z(n, 1, 2)
        fwd_x(n, 0, 3)
        fwd_z(n, 1, 3)
        acc(n, 0, 2)
        fwd_x(n, 1, 0)
        acc(n, 0, 3)
        y_step(n, 0)
        fwd_x(n, 1, 1)
        acc(n, 1, 0)
        fwd_x(n, 1, 2)
        acc(n, 1, 1)
        fwd_x(n, 1, 3)
        acc(n, 1, 2)
        acc(n, 1, 3)
        y_step(n, 1)

    for g in range(4):
        s_step(NT - 1, g)

    for copy in sends:
        copy.wait_send()
    for copy in outs:
        copy.wait()


def solution(mesh):
    n_slab = mesh.shape["slab"]

    def shards(rhs, front, pend, iidx, a, inv, oidx, b, finv):
        smem = pl.BlockSpec(memory_space=pltpu.SMEM)
        anyw = pl.BlockSpec(memory_space=pl.ANY)
        dma = pltpu.SemaphoreType.DMA
        half = pltpu.VMEM((NF, BL, HW), BF)
        sol, fro = pl.pallas_call(
            lambda *refs: kernel(n_slab, *refs),
            name="substitution",
            out_shape=(
                jax.ShapeDtypeStruct((NI, BL, NT * CW), BF),
                jax.ShapeDtypeStruct((NJ, BL, NT * CW), BF),
            ),
            in_specs=[smem, smem] + [anyw] * 7,
            out_specs=(anyw, anyw),
            scratch_shapes=[half] * 6
            + [
                pltpu.VMEM((NI, NL + 1, BL, BL), BF),
                pltpu.VMEM((NI, BL, BL), BF),
                pltpu.VMEM((NJ, NK, BL, BL), BF),
                pltpu.VMEM((NJ, BL, BL), BF),
                pltpu.VMEM((NT, NI, BL, CW), BF),
                pltpu.VMEM((NJ, BL, NT * CW), BF),
                pltpu.VMEM((NT, NI, BL, CW), F32),
                pltpu.VMEM((NT, NI, BL, CW), BF),
                pltpu.VMEM((NF, NJ * BL, BL), BF),
                pltpu.VMEM((NT, 2, NJ * BL, HW), F32),
                pltpu.VMEM((NT, 2, NJ, BL, HW), BF),
                pltpu.VMEM((NT - 1, 2, NJ, BL, HW), BF),
                pltpu.VMEM((NT, NI, BL, CW), BF),
                pltpu.SMEM((NI * NF,), jnp.int32),
                dma((16,)),
                dma((32,)),
            ]
            + [dma((NT, 2, NJ))] * 8,
            compiler_params=pltpu.CompilerParams(
                collective_id=0,
                has_side_effects=True,
                vmem_limit_bytes=56 * 1024 * 1024,
            ),
        )(
            iidx,
            oidx,
            rhs.reshape(NI, BL, NT * CW),
            front.reshape(NJ, BL, NT * CW),
            pend.reshape(NJ, BL, CW),
            a,
            inv,
            b,
            finv,
        )
        return sol.reshape(NI * BL, NT * CW), fro.reshape(NJ * BL, NT * CW)

    both = ("slab", "sub")
    two = P(both, None)
    return jax.shard_map(
        shards,
        mesh=mesh,
        in_specs=(
            two,
            two,
            two,
            two,
            P(both, None, None, None),
            P(both, None, None),
            two,
            P(both, None, None, None),
            P(both, None, None),
        ),
        out_specs=(two, two),
        check_vma=False,
    )
```

```python
import jax
import jax.numpy as jnp
from jax import lax
from jax.experimental import pallas as pl
from jax.experimental.pallas import tpu as pltpu
from jax.sharding import PartitionSpec as P

BF = jnp.bfloat16
F32 = jnp.float32
MESH = pl.DeviceIdType.MESH
BL = 128
NI = 16
NL = 6
NJ = 4
NK = 8
NF = 16
NT = 3
CW = 256
HW = 128


def lanes(parts):
    return jnp.concatenate(parts, axis=1)


def rows(parts):
    return jnp.concatenate(parts, axis=0)


def mm(a, b):
    return jnp.dot(a, b, preferred_element_type=F32)


def kernel(
    n_slab,
    iidx_h,
    oidx_h,
    rhs_h,
    front_h,
    pend_h,
    a_h,
    inv_h,
    b_h,
    finv_h,
    sol,
    fro,
    f00,
    f01,
    f10,
    f11,
    f20,
    f21,
    a,
    inv,
    b,
    finv,
    rhs,
    front,
    p32,
    pbf,
    cmat,
    w,
    ysend,
    iidx,
    oidx,
    pos,
    load_sem,
    send_z,
    recv_z,
    send_s,
    recv_s,
    send_x,
    recv_x,
    send_xs,
    recv_xs,
):
    fr = ((f00, f01), (f10, f11), (f20, f21))
    slab = lax.axis_index("slab")
    sub = lax.axis_index("sub")
    sib = sub + 1 - 2 * (sub % 2)
    xp = (sub + 2) % 4
    to_sub = (sub + 2 * ((slab + 1) % 8 == 0).astype(jnp.int32)) % 4
    from_sub = (sub + 2 * (slab % 8 == 0).astype(jnp.int32)) % 4
    gives = slab < n_slab - 1
    takes = slab > 0
    sib_id = (slab, sib)
    x_id = (slab, xp)
    next_id = ((slab + 1) % n_slab, to_sub)
    prev_id = ((slab + n_slab - 1) % n_slab, from_sub)

    barrier = pltpu.get_barrier_semaphore()
    for peer in (sib_id, x_id):
        pl.semaphore_signal(barrier, inc=1, device_id=peer, device_id_type=MESH)

    @pl.when(takes)
    def _():
        pl.semaphore_signal(barrier, inc=1, device_id=prev_id, device_id_type=MESH)

    def share(t):
        base = sub if t == 0 else from_sub
        one = base + 1 - 2 * (base % 2)
        return (base, one, (base + 2) % 4, (one + 2) % 4)

    loads = []

    def load(src, dst):
        copy = pltpu.make_async_copy(src, dst, load_sem.at[len(loads)])
        copy.start()
        loads.append(copy)
        return copy

    ld_idx = [load(iidx_h, iidx), load(oidx_h, oidx)]
    ld_inv = load(inv_h, inv)
    ld_a = [
        load(a_h.at[pl.ds(4 * g, 4)], a.at[pl.ds(4 * g, 4), pl.ds(0, NL)])
        for g in range(4)
    ]
    ld_finv = load(finv_h, finv)
    ld_b = load(b_h, b)
    ld_r = [load(rhs_h.at[:, :, 0:CW], rhs.at[0])]
    own = [
        load(
            pend_h.at[:, :, c * HW : (c + 1) * HW],
            fr[0][c].at[pl.ds(4 * sub, 4)],
        )
        for c in range(2)
    ]
    ld_g = load(front_h, front)
    for t in range(1, NT):
        ld_r.append(load(rhs_h.at[:, :, t * CW : (t + 1) * CW], rhs.at[t]))

    sends = []

    def send(when, src, dst, ssem, rsem, ssem_at, peer):
        copy = pltpu.make_async_remote_copy(
            src_ref=src,
            dst_ref=dst,
            send_sem=ssem.at[ssem_at],
            recv_sem=rsem.at[ssem_at],
            device_id=peer,
            device_id_type=MESH,
        )
        copy.start()
        sends.append((when, ssem, ssem_at))

    def gated(when, body):
        if when is None:
            body()
        else:
            pl.when(when)(body)

    def taken(t):
        return takes if t else None

    def arrived(t, c, which, p, rsem):
        block = fr[t][c].at[4 * share(t)[which] + p]
        pltpu.make_async_copy(block, block, rsem.at[t, c, p]).wait()

    def greet():
        pl.semaphore_wait(barrier, 2 + gives.astype(jnp.int32))

    def gather():
        for c in range(2):
            for p in range(NJ):
                src = pend_h.at[p, :, c * HW : (c + 1) * HW]
                dst = fr[0][c].at[4 * share(0)[0] + p]
                send(None, src, dst, send_x, recv_x, (0, c, p), x_id)
            for p in range(NJ):
                src = pend_h.at[p, :, c * HW : (c + 1) * HW]
                dst = fr[0][c].at[4 * share(0)[0] + p]
                send(None, src, dst, send_s, recv_s, (0, c, p), sib_id)

    def fwd_z(t, c, *ps):
        def body():
            for p in ps:
                arrived(t, c, 0, p, recv_z)
                block = fr[t][c].at[4 * share(t)[0] + p]
                at = (t, c, p)
                send(takes, block, block, send_x, recv_x, at, x_id)
                send(takes, block, block, send_s, recv_s, at, sib_id)

        gated(taken(t), body)

    def fwd_x(t, c, *ps):
        def body():
            for p in ps:
                arrived(t, c, 2, p, recv_x)
                block = fr[t][c].at[4 * share(t)[2] + p]
                at = (t, c, p)
                send(taken(t), block, block, send_xs, recv_xs, at, sib_id)

        gated(taken(t), body)

    def arr_s(t, c):
        def body():
            for p in range(NJ):
                arrived(t, c, 1, p, recv_s)

        gated(taken(t), body)

    def arr_xs(t, c):
        def body():
            for p in range(NJ):
                arrived(t, c, 3, p, recv_xs)

        gated(taken(t), body)

    def place(i, carry):
        own_links = [iidx[k, i] for k in range(NL)]
        for f in range(NF):
            at = jnp.int32(NL)
            for k in range(NL):
                at = jnp.where(own_links[k] == f, jnp.int32(k), at)
            pos[i * NF + f] = at
        return carry

    def places():
        for copy in ld_idx:
            copy.wait()
        lax.fori_loop(0, NI, place, 0)
        for i in range(NI):
            a[i, NL] = jnp.zeros((BL, BL), BF)

        @pl.when(slab == 0)
        def _():
            for t in range(1, NT):
                for c in range(2):
                    fr[t][c][...] = jnp.zeros((NF, BL, HW), BF)

    def a_wait(g):
        if g == 0:
            ld_inv.wait()
        ld_a[g].wait()

    def a_step(g):
        for i in range(4 * g, 4 * g + 4):
            for m in range(0, NL, 2):
                o = mm(inv[i], lanes([a[i, m], a[i, m + 1]]))
                o = (-o).astype(BF)
                a[i, m] = o[:, :BL]
                a[i, m + 1] = o[:, BL:]

    def b_wait():
        ld_finv.wait()
        ld_b.wait()

    def b_step():
        for j in range(NJ):
            for m in range(0, NK, 2):
                o = mm(finv[j], lanes([b[j, m], b[j, m + 1]]))
                o = (-o).astype(BF)
                b[j, m] = o[:, :BL]
                b[j, m + 1] = o[:, BL:]

    def c_step(*gs):
        for g in gs:
            for j in range(NJ):
                tiles = []
                for k in range(NK):
                    at = oidx[j, k]
                    tiles.append(
                        lanes(
                            [
                                a[at, pos[at * NF + 2 * g]],
                                a[at, pos[at * NF + 2 * g + 1]],
                            ]
                        )
                    )
                o = mm(lanes([b[j, k] for k in range(NK)]), rows(tiles)).astype(BF)
                cmat[2 * g, pl.ds(j * BL, BL)] = o[:, :BL]
                cmat[2 * g + 1, pl.ds(j * BL, BL)] = o[:, BL:]

    def p_step(t):
        ld_r[t].wait()
        for i in range(NI):
            o = mm(inv[i], rhs[t, i])
            p32[t, i] = o
            if t:
                pbf[t - 1, i] = o.astype(BF)

    def front_left(j):
        return lanes([finv[j]] + [b[j, k] for k in range(NK)])

    def w_step(t):
        for j in range(NJ):
            right = rows(
                [front[j, :, t * CW : (t + 1) * CW]]
                + [pbf[t - 1, oidx[j, k]] for k in range(NK)]
            )
            o = mm(front_left(j), right)
            w[t - 1, 0, pl.ds(j * BL, BL)] = o[:, :HW]
            w[t - 1, 1, pl.ds(j * BL, BL)] = o[:, HW:]

    def acc(t, c, *which):
        shares = [share(t)[n] for n in which]
        left = lanes([cmat[4 * sh + r] for sh in shares for r in range(4)])
        right = rows([fr[t][c][pl.ds(4 * sh, 4)].reshape(4 * BL, HW) for sh in shares])
        return w[t - 1, c] + mm(left, right)

    def acc3(t, c):
        arr_s(t, c)
        w[t - 1, c] = acc(t, c, 0, 1, 2)

    def pass_on(t, c):
        def body():
            for p in range(NJ):
                at = (t + 1, c, p)
                send(
                    gives,
                    ysend.at[t, c, p],
                    fr[t + 1][c].at[4 * sub + p],
                    send_z,
                    recv_z,
                    at,
                    next_id,
                )

        gated(gives, body)

    def columns(t, c):
        return slice(t * CW + c * HW, t * CW + (c + 1) * HW)

    def y_step(t, c):
        arr_xs(t, c)
        value = acc(t, c, 3).astype(BF).reshape(NJ, BL, HW)
        if t + 1 < NT:
            ysend[t, c] = value
            pass_on(t, c)
        fro[:, :, columns(t, c)] = value

    def s0_wait(c):
        own[c].wait()
        arr_s(0, c)
        arr_xs(0, c)

    def s0_step(c, *ids):
        for i in ids:
            left = lanes([a[i, k] for k in range(NL)])
            right = rows([fr[0][c][iidx[k, i]] for k in range(NL)])
            base = p32[0, i, :, c * HW : (c + 1) * HW]
            sol[i, :, columns(0, c)] = (base + mm(left, right)).astype(BF)

    def y0_step(c):
        for j in range(NJ):
            right = rows(
                [front[j, :, columns(0, c)]]
                + [sol[oidx[j, k], :, columns(0, c)] for k in range(NK)]
            )
            value = mm(front_left(j), right).astype(BF)
            ysend[0, c, j] = value
            fro[j, :, columns(0, c)] = value
        pass_on(0, c)

    def s_step(t, *ids):
        for i in ids:
            left = lanes([a[i, k] for k in range(NL)])
            right = rows(
                [
                    lanes([fr[t][0][iidx[k, i]], fr[t][1][iidx[k, i]]])
                    for k in range(NL)
                ]
            )
            o = (p32[t, i] + mm(left, right)).astype(BF)
            sol[i, :, t * CW : (t + 1) * CW] = o

    places()
    greet()
    gather()
    for g in range(4):
        a_wait(g)
        a_step(g)
    b_wait()
    b_step()
    p_step(0)
    fwd_x(0, 0, 0)
    c_step(0)
    fwd_x(0, 0, 1)
    c_step(1)
    fwd_x(0, 0, 2, 3)
    c_step(2)
    fwd_x(0, 1, 0)
    s0_wait(0)
    s0_step(0, *range(0, 8))
    fwd_x(0, 1, 1, 2)
    s0_step(0, *range(8, 16))
    fwd_x(0, 1, 3)
    ld_g.wait()
    y0_step(0)
    s0_wait(1)
    s0_step(1, *range(16))
    y0_step(1)
    c_step(3, 4)
    fwd_z(1, 0, 0, 1)
    c_step(5)
    fwd_z(1, 0, 2, 3)
    c_step(6)
    fwd_z(1, 1, 0, 1)
    c_step(7)
    fwd_z(1, 1, 2)
    p_step(1)
    fwd_z(1, 1, 3)
    fwd_x(1, 0, 0, 1)
    w_step(1)
    fwd_x(1, 0, 2, 3)
    acc3(1, 0)
    fwd_x(1, 1, 0)
    y_step(1, 0)
    fwd_x(1, 1, 1, 2, 3)
    acc3(1, 1)
    y_step(1, 1)
    s_step(1, *range(0, 8))
    fwd_z(2, 0, 0, 1)
    s_step(1, *range(8, 12))
    fwd_z(2, 0, 2, 3)
    s_step(1, *range(12, 16))
    fwd_z(2, 1, 0, 1)
    p_step(2)
    fwd_z(2, 1, 2, 3)
    w_step(2)
    fwd_x(2, 0, 0, 1, 2, 3)
    acc3(2, 0)
    fwd_x(2, 1, 0)
    y_step(2, 0)
    fwd_x(2, 1, 1, 2, 3)
    acc3(2, 1)
    y_step(2, 1)
    s_step(2, *range(16))

    def finish():
        for when in (None, takes, gives):
            sent = [(sem, at) for cond, sem, at in sends if cond is when]

            def body(sent=sent):
                for sem, at in sent:
                    block = ysend.at[0, 0, 0]
                    pltpu.make_async_copy(block, block, sem.at[at]).wait()

            gated(when, body)

    finish()


def solution(mesh):
    n_slab = mesh.shape["slab"]

    def shards(rhs, front, pend, iidx, a, inv, oidx, b, finv):
        vmem = pl.BlockSpec(memory_space=pltpu.VMEM)
        hbm = pl.BlockSpec(memory_space=pltpu.HBM)
        dma = pltpu.SemaphoreType.DMA
        half = pltpu.VMEM((NF, BL, HW), BF)
        sol, fro = pl.pallas_call(
            lambda *refs: kernel(n_slab, *refs),
            name="substitution",
            out_shape=(
                pltpu.VMEM((NI, BL, NT * CW), BF),
                pltpu.VMEM((NJ, BL, NT * CW), BF),
            ),
            in_specs=[hbm] * 9,
            out_specs=(vmem, vmem),
            scratch_shapes=[half] * 6
            + [
                pltpu.VMEM((NI, NL + 1, BL, BL), BF),
                pltpu.VMEM((NI, BL, BL), BF),
                pltpu.VMEM((NJ, NK, BL, BL), BF),
                pltpu.VMEM((NJ, BL, BL), BF),
                pltpu.VMEM((NT, NI, BL, CW), BF),
                pltpu.VMEM((NJ, BL, NT * CW), BF),
                pltpu.VMEM((NT, NI, BL, CW), F32),
                pltpu.VMEM((NT - 1, NI, BL, CW), BF),
                pltpu.VMEM((NF, NJ * BL, BL), BF),
                pltpu.VMEM((NT - 1, 2, NJ * BL, HW), F32),
                pltpu.VMEM((NT - 1, 2, NJ, BL, HW), BF),
                pltpu.SMEM((NL, NI), jnp.int32),
                pltpu.SMEM((NJ, NK), jnp.int32),
                pltpu.SMEM((NI * NF,), jnp.int32),
                dma((16,)),
            ]
            + [dma((NT, 2, NJ))] * 8,
            compiler_params=pltpu.CompilerParams(
                collective_id=0,
                has_side_effects=True,
                vmem_limit_bytes=36 * 1024 * 1024,
            ),
        )(
            *(
                pltpu.with_memory_space_constraint(x, pltpu.HBM)
                for x in (
                    iidx.T,
                    oidx,
                    rhs.reshape(NI, BL, NT * CW),
                    front.reshape(NJ, BL, NT * CW),
                    pend.reshape(NJ, BL, CW),
                    a,
                    inv,
                    b,
                    finv,
                )
            )
        )
        return sol.reshape(NI * BL, NT * CW), fro.reshape(NJ * BL, NT * CW)

    both = ("slab", "sub")
    two = P(both, None)
    return jax.shard_map(
        shards,
        mesh=mesh,
        in_specs=(
            two,
            two,
            two,
            two,
            P(both, None, None, None),
            P(both, None, None),
            two,
            P(both, None, None, None),
            P(both, None, None),
        ),
        out_specs=(two, two),
        check_vma=False,
    )
```

```python
import jax
import jax.numpy as jnp
from jax import lax
from jax.experimental import pallas as pl
from jax.experimental.pallas import tpu as pltpu
from jax.sharding import PartitionSpec as P

BF = jnp.bfloat16
F32 = jnp.float32
MESH = pl.DeviceIdType.MESH
BL = 128
NI = 16
NL = 6
NJ = 4
NK = 8
NF = 16
NT = 3
CW = 256
HW = 128


def lanes(parts):
    return jnp.concatenate(parts, axis=1)


def rows(parts):
    return jnp.concatenate(parts, axis=0)


def mm(a, b):
    return jnp.dot(a, b, preferred_element_type=F32)


def source_of(slab, sub):
    return (sub + 2 * (slab % 8 == 0).astype(jnp.int32)) % 4


def shares_of(base):
    one = base + 1 - 2 * (base % 2)
    return (base, one, (base + 2) % 4, (one + 2) % 4)


def columns(t, c):
    return slice(t * CW + c * HW, t * CW + (c + 1) * HW)


def dense(cmat, front_half, shares):
    left = lanes([cmat[4 * sh + r] for sh in shares for r in range(4)])
    right = rows([front_half[pl.ds(4 * sh, 4)].reshape(4 * BL, HW) for sh in shares])
    return mm(left, right)


def interior(a, halves, iidx, i):
    left = lanes([a[i, k] for k in range(NL)])
    right = rows([lanes([half[iidx[k, i]] for half in halves]) for k in range(NL)])
    return mm(left, right)


def kernel(
    n_slab,
    iidx_h,
    oidx_h,
    rhs_h,
    front_h,
    pend_h,
    a_h,
    inv_h,
    b_h,
    finv_h,
    sol,
    fro,
    f20,
    f21,
    a,
    p2,
    cmat,
    w2,
    f00,
    f01,
    f10,
    f11,
    inv,
    b,
    finv,
    rhs,
    front,
    p32,
    pbf,
    w1,
    ysend,
    iidx,
    oidx,
    pos,
    load_sem,
    sent,
    recv_z,
    recv_x,
    recv_s,
    recv_xs,
):
    fr = ((f00, f01), (f10, f11), (f20, f21))
    w = (None, w1, w2)
    slab = lax.axis_index("slab")
    sub = lax.axis_index("sub")
    sib = sub + 1 - 2 * (sub % 2)
    xp = (sub + 2) % 4
    to_sub = (sub + 2 * ((slab + 1) % 8 == 0).astype(jnp.int32)) % 4
    from_sub = source_of(slab, sub)
    gives = slab < n_slab - 1
    takes = slab > 0
    sib_id = (slab, sib)
    x_id = (slab, xp)
    next_id = ((slab + 1) % n_slab, to_sub)
    prev_id = ((slab + n_slab - 1) % n_slab, from_sub)

    barrier = pltpu.get_barrier_semaphore()
    for peer in (sib_id, x_id):
        pl.semaphore_signal(barrier, inc=1, device_id=peer, device_id_type=MESH)

    @pl.when(takes)
    def _():
        pl.semaphore_signal(barrier, inc=1, device_id=prev_id, device_id_type=MESH)

    def share(t):
        return shares_of(sub if t == 0 else from_sub)

    loads = []

    def load(src, dst):
        copy = pltpu.make_async_copy(src, dst, load_sem.at[len(loads)])
        copy.start()
        loads.append(copy)
        return copy

    ld_idx = [load(iidx_h, iidx), load(oidx_h, oidx)]
    ld_inv = load(inv_h, inv)
    ld_a = [
        load(a_h.at[pl.ds(4 * g, 4)], a.at[pl.ds(4 * g, 4), pl.ds(0, NL)])
        for g in range(4)
    ]
    ld_finv = load(finv_h, finv)
    ld_b = load(b_h, b)
    ld_r = [load(rhs_h.at[:, :, 0:CW], rhs.at[0])]
    own = [
        load(
            pend_h.at[:, :, c * HW : (c + 1) * HW],
            fr[0][c].at[pl.ds(4 * sub, 4)],
        )
        for c in range(2)
    ]
    ld_g = load(front_h, front)

    def late_loads():
        for t in range(1, NT):
            ld_r.append(load(rhs_h.at[:, :, t * CW : (t + 1) * CW], rhs.at[t]))

    def send(src, dst, kind, got, peer):
        pltpu.make_async_remote_copy(
            src_ref=src,
            dst_ref=dst,
            send_sem=sent.at[kind],
            recv_sem=got,
            device_id=peer,
            device_id_type=MESH,
        ).start()

    def gated(when, body):
        if when is None:
            body()
        else:
            pl.when(when)(body)

    def taken(t):
        return takes if t else None

    def arrived(t, c, which, p, got):
        block = fr[t][c].at[4 * share(t)[which] + p]
        pltpu.make_async_copy(block, block, got).wait()

    def arrived_whole(t, c, which, got):
        def body():
            block = fr[t][c].at[pl.ds(4 * share(t)[which], 4)]
            pltpu.make_async_copy(block, block, got).wait()

        gated(taken(t), body)

    def greet():
        pl.semaphore_wait(barrier, 2 + gives.astype(jnp.int32))

    def gather(c):
        for p in range(NJ):
            src = pend_h.at[p, :, c * HW : (c + 1) * HW]
            dst = fr[0][c].at[4 * sub + p]
            send(src, dst, 0, recv_x.at[0, c, p], x_id)
        for p in range(NJ):
            src = pend_h.at[p, :, c * HW : (c + 1) * HW]
            dst = fr[0][c].at[4 * sub + p]
            send(src, dst, 0, recv_s.at[0, c], sib_id)

    def fwd_z(t, c, *ps):
        def body():
            for p in ps:
                got = recv_z.at[t - 1, c, p]
                arrived(t, c, 0, p, got)
                block = fr[t][c].at[4 * share(t)[0] + p]
                send(block, block, 1, recv_x.at[t, c, p], x_id)
                send(block, block, 1, recv_s.at[t, c], sib_id)

        gated(taken(t), body)

    def fwd_x(t, c, *ps):
        def body():
            for p in ps:
                arrived(t, c, 2, p, recv_x.at[t, c, p])
                block = fr[t][c].at[4 * share(t)[2] + p]
                send(block, block, min(t, 1), recv_xs.at[t, c], sib_id)

        gated(taken(t), body)

    def arr_s(t, c):
        arrived_whole(t, c, 1, recv_s.at[t, c])

    def arr_xs(t, c):
        arrived_whole(t, c, 3, recv_xs.at[t, c])

    def place(i, carry):
        own_links = [iidx[k, i] for k in range(NL)]
        for f in range(NF):
            at = jnp.int32(NL)
            for k in range(NL):
                at = jnp.where(own_links[k] == f, jnp.int32(k), at)
            pos[i * NF + f] = at
        return carry

    def places():
        for copy in ld_idx:
            copy.wait()
        lax.fori_loop(0, NI, place, 0)
        for i in range(NI):
            a[i, NL] = jnp.zeros((BL, BL), BF)

        @pl.when(slab == 0)
        def _():
            for t in range(1, NT):
                for c in range(2):
                    fr[t][c][...] = jnp.zeros((NF, BL, HW), BF)

    def a_wait(g):
        if g == 0:
            ld_inv.wait()
        ld_a[g].wait()

    def a_step(g):
        for i in range(4 * g, 4 * g + 4):
            for m in range(0, NL, 2):
                o = mm(inv[i], lanes([a[i, m], a[i, m + 1]]))
                o = (-o).astype(BF)
                a[i, m] = o[:, :BL]
                a[i, m + 1] = o[:, BL:]

    def b_wait():
        ld_finv.wait()
        ld_b.wait()

    def b_step():
        for j in range(NJ):
            for m in range(0, NK, 2):
                o = mm(finv[j], lanes([b[j, m], b[j, m + 1]]))
                o = (-o).astype(BF)
                b[j, m] = o[:, :BL]
                b[j, m + 1] = o[:, BL:]

    def c_step(*gs):
        for g in gs:
            for j in range(NJ):
                tiles = []
                for k in range(NK):
                    at = oidx[j, k]
                    tiles.append(
                        lanes(
                            [
                                a[at, pos[at * NF + 2 * g]],
                                a[at, pos[at * NF + 2 * g + 1]],
                            ]
                        )
                    )
                o = mm(lanes([b[j, k] for k in range(NK)]), rows(tiles)).astype(BF)
                cmat[2 * g, pl.ds(j * BL, BL)] = o[:, :BL]
                cmat[2 * g + 1, pl.ds(j * BL, BL)] = o[:, BL:]

    def p_step(t):
        ld_r[t].wait()
        for i in range(NI):
            o = mm(inv[i], rhs[t, i])
            if t < 2:
                p32[t, i] = o
            else:
                p2[i] = o
            if t:
                pbf[t - 1, i] = o.astype(BF)

    def front_left(j):
        return lanes([finv[j]] + [b[j, k] for k in range(NK)])

    def w_step(t):
        for j in range(NJ):
            right = rows(
                [front[j, :, t * CW : (t + 1) * CW]]
                + [pbf[t - 1, oidx[j, k]] for k in range(NK)]
            )
            o = mm(front_left(j), right)
            w[t][0, pl.ds(j * BL, BL)] = o[:, :HW]
            w[t][1, pl.ds(j * BL, BL)] = o[:, HW:]

    def acc2(t, c):
        arr_s(t, c)
        sh = share(t)
        w[t][c] = w[t][c] + dense(cmat, fr[t][c], sh[:2])

    def acc1(t, c):
        w[t][c] = w[t][c] + dense(cmat, fr[t][c], share(t)[2:3])

    def pass_on(t, c, *ps):
        def body():
            for p in ps:
                dst = fr[t + 1][c].at[4 * sub + p]
                got = recv_z.at[t, c, p]
                send(ysend.at[t, c, p], dst, 2, got, next_id)

        gated(gives, body)

    def y_step(t, c):
        arr_xs(t, c)
        sh = share(t)[3]
        right = fr[t][c][pl.ds(4 * sh, 4)].reshape(4 * BL, HW)
        for j in (0, 2):
            at = pl.ds(j * BL, 2 * BL)
            left = lanes([cmat[4 * sh + r, at] for r in range(4)])
            value = (w[t][c, at] + mm(left, right)).astype(BF).reshape(2, BL, HW)
            if t + 1 < NT:
                ysend[t, c, pl.ds(j, 2)] = value
                pass_on(t, c, j, j + 1)
            fro[j : j + 2, :, columns(t, c)] = value

    def s0_wait(c):
        own[c].wait()
        arr_s(0, c)
        arr_xs(0, c)

    def s0_step(c, *ids):
        for i in ids:
            base = p32[0, i, :, c * HW : (c + 1) * HW]
            o = base + interior(a, fr[0][c : c + 1], iidx, i)
            sol[i, :, columns(0, c)] = o.astype(BF)

    def y0_step(c):
        for j in range(NJ):
            right = rows(
                [front[j, :, columns(0, c)]]
                + [sol[oidx[j, k], :, columns(0, c)] for k in range(NK)]
            )
            value = mm(front_left(j), right).astype(BF)
            ysend[0, c, j] = value
            fro[j, :, columns(0, c)] = value
            if j % 2:
                pass_on(0, c, j - 1, j)

    def s_step(t, *ids):
        for i in ids:
            o = (p32[t, i] + interior(a, fr[t], iidx, i)).astype(BF)
            sol[i, :, t * CW : (t + 1) * CW] = o

    greet()
    gather(0)
    places()
    for g in range(4):
        a_wait(g)
        a_step(g)
    gather(1)
    late_loads()
    b_wait()
    b_step()
    p_step(0)
    fwd_x(0, 0, 0)
    c_step(0)
    fwd_x(0, 0, 1)
    c_step(1)
    fwd_x(0, 0, 2)
    ld_g.wait()
    fwd_x(0, 0, 3)
    c_step(2, 3)
    fwd_x(0, 1, 0)
    s0_wait(0)
    s0_step(0, *range(16))
    y0_step(0)
    fwd_x(0, 1, 1, 2, 3)
    c_step(4, 5)
    s0_wait(1)
    s0_step(1, *range(16))
    y0_step(1)
    fwd_z(1, 0, 0)
    c_step(6)
    fwd_z(1, 0, 1)
    c_step(7)
    fwd_z(1, 0, 2)
    p_step(1)
    fwd_z(1, 0, 3)
    w_step(1)
    fwd_z(1, 1, 0)
    acc2(1, 0)
    fwd_x(1, 0, 0)
    fwd_z(1, 1, 1)
    fwd_x(1, 0, 1)
    fwd_z(1, 1, 2)
    fwd_x(1, 0, 2)
    fwd_z(1, 1, 3)
    fwd_x(1, 0, 3)
    acc1(1, 0)
    fwd_x(1, 1, 0)
    y_step(1, 0)
    fwd_x(1, 1, 1)
    acc2(1, 1)
    fwd_x(1, 1, 2, 3)
    acc1(1, 1)
    y_step(1, 1)
    fwd_z(2, 0, 0)
    s_step(1, *range(0, 4))
    fwd_z(2, 0, 1)
    s_step(1, *range(4, 8))
    fwd_z(2, 0, 2)
    s_step(1, *range(8, 12))
    fwd_z(2, 0, 3)
    s_step(1, *range(12, 16))
    fwd_z(2, 1, 0)
    p_step(2)
    fwd_x(2, 0, 0)
    fwd_z(2, 1, 1)
    w_step(2)
    fwd_x(2, 0, 1)
    fwd_z(2, 1, 2)
    acc2(2, 0)
    fwd_x(2, 0, 2)
    fwd_z(2, 1, 3)
    fwd_x(2, 0, 3)
    acc1(2, 0)
    fwd_x(2, 1, 0)
    y_step(2, 0)
    fwd_x(2, 1, 1)
    acc2(2, 1)
    fwd_x(2, 1, 2, 3)
    acc1(2, 1)
    arr_xs(2, 1)

    def finish():
        def gone(kind, ref):
            pltpu.make_async_copy(ref, ref, sent.at[kind]).wait()

        gone(0, rhs.at[:, pl.ds(0, 4)])
        gated(takes, lambda: gone(1, rhs.at[:, pl.ds(0, 8)]))
        gated(gives, lambda: gone(2, ysend))

    finish()


def last(iidx_h, sol01, fro01, f20, f21, a, p2, cmat, w2, sol, fro, s, y, iidx, sem):
    moves = []

    def move(src, dst):
        copy = pltpu.make_async_copy(src, dst, sem.at[len(moves)])
        copy.start()
        moves.append(copy)
        return copy

    links = move(iidx_h, iidx)
    move(sol01, sol.at[:, :, : 2 * CW])
    cut = 2 * CW + HW
    move(fro01.at[:, :, :cut], fro.at[:, :, :cut])
    sh = shares_of(source_of(lax.axis_index("slab"), lax.axis_index("sub")))
    value = w2[1] + dense(cmat, f21, sh[3:])
    y[...] = value.astype(BF).reshape(NJ, BL, HW)
    move(y, fro.at[:, :, cut:])
    links.wait()
    for g in range(2):
        for i in range(8 * g, 8 * g + 8):
            s[i] = (p2[i] + interior(a, (f20, f21), iidx, i)).astype(BF)
        at = pl.ds(8 * g, 8)
        move(s.at[at], sol.at[at, :, 2 * CW :])
    for copy in moves[1:]:
        copy.wait()


def solution(mesh):
    n_slab = mesh.shape["slab"]

    def shards(rhs, front, pend, iidx, a, inv, oidx, b, finv):
        vmem = pl.BlockSpec(memory_space=pltpu.VMEM)
        hbm = pl.BlockSpec(memory_space=pltpu.HBM)
        dma = pltpu.SemaphoreType.DMA
        half = pltpu.VMEM((NF, BL, HW), BF)
        def in_hbm(x):
            return pltpu.with_memory_space_constraint(x, pltpu.HBM)

        def in_vmem(x):
            return pltpu.with_memory_space_constraint(x, pltpu.VMEM)

        iidx = in_hbm(iidx.T)
        made = pl.pallas_call(
            lambda *refs: kernel(n_slab, *refs),
            name="substitution",
            out_shape=(
                pltpu.VMEM((NI, BL, 2 * CW), BF),
                pltpu.VMEM((NJ, BL, NT * CW), BF),
                half,
                half,
                pltpu.VMEM((NI, NL + 1, BL, BL), BF),
                pltpu.VMEM((NI, BL, CW), F32),
                pltpu.VMEM((NF, NJ * BL, BL), BF),
                pltpu.VMEM((2, NJ * BL, HW), F32),
            ),
            in_specs=[hbm] * 9,
            out_specs=(vmem,) * 8,
            scratch_shapes=[half] * 4
            + [
                pltpu.VMEM((NI, BL, BL), BF),
                pltpu.VMEM((NJ, NK, BL, BL), BF),
                pltpu.VMEM((NJ, BL, BL), BF),
                pltpu.VMEM((NT, NI, BL, CW), BF),
                pltpu.VMEM((NJ, BL, NT * CW), BF),
                pltpu.VMEM((2, NI, BL, CW), F32),
                pltpu.VMEM((2, NI, BL, CW), BF),
                pltpu.VMEM((2, NJ * BL, HW), F32),
                pltpu.VMEM((2, 2, NJ, BL, HW), BF),
                pltpu.SMEM((NL, NI), jnp.int32),
                pltpu.SMEM((NJ, NK), jnp.int32),
                pltpu.SMEM((NI * NF,), jnp.int32),
                dma((15,)),
                dma((3,)),
                dma((NT - 1, 2, NJ)),
                dma((NT, 2, NJ)),
                dma((NT, 2)),
                dma((NT, 2)),
            ],
            compiler_params=pltpu.CompilerParams(
                collective_id=0,
                has_side_effects=True,
                vmem_limit_bytes=30 * 1024 * 1024,
            ),
        )(
            iidx,
            *(
                in_hbm(x)
                for x in (
                    oidx,
                    rhs.reshape(NI, BL, NT * CW),
                    front.reshape(NJ, BL, NT * CW),
                    pend.reshape(NJ, BL, CW),
                    a,
                    inv,
                    b,
                    finv,
                )
            )
        )
        sol, fro = pl.pallas_call(
            last,
            name="last",
            out_shape=(
                pltpu.HBM((NI, BL, NT * CW), BF),
                pltpu.HBM((NJ, BL, NT * CW), BF),
            ),
            in_specs=[hbm] + [vmem] * 8,
            out_specs=(hbm, hbm),
            scratch_shapes=[
                pltpu.VMEM((NI, BL, CW), BF),
                pltpu.VMEM((NJ, BL, HW), BF),
                pltpu.SMEM((NL, NI), jnp.int32),
                dma((6,)),
            ],
            compiler_params=pltpu.CompilerParams(
                vmem_limit_bytes=30 * 1024 * 1024,
            ),
        )(iidx, *(in_vmem(x) for x in made))
        return sol.reshape(NI * BL, NT * CW), fro.reshape(NJ * BL, NT * CW)

    both = ("slab", "sub")
    two = P(both, None)
    return jax.shard_map(
        shards,
        mesh=mesh,
        in_specs=(
            two,
            two,
            two,
            two,
            P(both, None, None, None),
            P(both, None, None),
            two,
            P(both, None, None, None),
            P(both, None, None),
        ),
        out_specs=(two, two),
        check_vma=False,
    )
```

```python
import jax
import jax.numpy as jnp
from jax import lax
from jax.experimental import pallas as pl
from jax.experimental.pallas import tpu as pltpu
from jax.sharding import PartitionSpec as P

BF = jnp.bfloat16
F32 = jnp.float32
MESH = pl.DeviceIdType.MESH
BL = 128
NI = 16
NL = 6
NJ = 4
NK = 8
NF = 16
NT = 3
CW = 256
HW = 128


def lanes(parts):
    return jnp.concatenate(parts, axis=1)


def rows(parts):
    return jnp.concatenate(parts, axis=0)


def mm(a, b):
    return jnp.dot(a, b, preferred_element_type=F32)


def source_of(slab, sub):
    return (sub + 2 * (slab % 8 == 0).astype(jnp.int32)) % 4


def shares_of(base):
    one = base + 1 - 2 * (base % 2)
    return (base, one, (base + 2) % 4, (one + 2) % 4)


def columns(t, c):
    return slice(t * CW + c * HW, t * CW + (c + 1) * HW)


def dense(cmat, front_half, shares):
    left = lanes([cmat[4 * sh + r] for sh in shares for r in range(4)])
    right = rows([front_half[pl.ds(4 * sh, 4)].reshape(4 * BL, HW) for sh in shares])
    return mm(left, right)


def interior(a, halves, iidx, i):
    left = lanes([a[i, k] for k in range(NL)])
    right = rows([lanes([half[iidx[k, i]] for half in halves]) for k in range(NL)])
    return mm(left, right)


def kernel(
    n_slab,
    iidx_h,
    oidx_h,
    rhs_h,
    front_h,
    pend_h,
    a_h,
    inv_h,
    b_h,
    finv_h,
    sol,
    fro,
    f21,
    a,
    p2,
    cmat,
    w2,
    f00,
    f01,
    f10,
    f11,
    f20,
    inv,
    b,
    finv,
    rhs,
    front,
    p32,
    pbf,
    w1,
    ysend,
    iidx,
    oidx,
    pos,
    load_sem,
    sent,
    recv_z,
    recv_x,
    recv_s,
    recv_xs,
):
    fr = ((f00, f01), (f10, f11), (f20, f21))
    w = (None, w1, w2)
    slab = lax.axis_index("slab")
    sub = lax.axis_index("sub")
    sib = sub + 1 - 2 * (sub % 2)
    xp = (sub + 2) % 4
    to_sub = (sub + 2 * ((slab + 1) % 8 == 0).astype(jnp.int32)) % 4
    from_sub = source_of(slab, sub)
    gives = slab < n_slab - 1
    takes = slab > 0
    sib_id = (slab, sib)
    x_id = (slab, xp)
    next_id = ((slab + 1) % n_slab, to_sub)
    prev_id = ((slab + n_slab - 1) % n_slab, from_sub)

    barrier = pltpu.get_barrier_semaphore()
    for peer in (sib_id, x_id):
        pl.semaphore_signal(barrier, inc=1, device_id=peer, device_id_type=MESH)

    @pl.when(takes)
    def _():
        pl.semaphore_signal(barrier, inc=1, device_id=prev_id, device_id_type=MESH)

    def share(t):
        return shares_of(sub if t == 0 else from_sub)

    loads = []

    def load(src, dst):
        copy = pltpu.make_async_copy(src, dst, load_sem.at[len(loads)])
        copy.start()
        loads.append(copy)
        return copy

    ld_idx = [load(iidx_h, iidx), load(oidx_h, oidx)]
    ld_inv = load(inv_h, inv)
    ld_a = [
        load(a_h.at[pl.ds(4 * g, 4)], a.at[pl.ds(4 * g, 4), pl.ds(0, NL)])
        for g in range(4)
    ]
    ld_finv = load(finv_h, finv)
    ld_b = load(b_h, b)
    ld_r = [load(rhs_h.at[:, :, 0:CW], rhs.at[0])]
    own = [
        load(
            pend_h.at[:, :, c * HW : (c + 1) * HW],
            fr[0][c].at[pl.ds(4 * sub, 4)],
        )
        for c in range(2)
    ]
    ld_g = load(front_h, front)

    def late_loads():
        for t in range(1, NT):
            ld_r.append(load(rhs_h.at[:, :, t * CW : (t + 1) * CW], rhs.at[t]))

    def send(src, dst, kind, got, peer):
        pltpu.make_async_remote_copy(
            src_ref=src,
            dst_ref=dst,
            send_sem=sent.at[kind],
            recv_sem=got,
            device_id=peer,
            device_id_type=MESH,
        ).start()

    def gated(when, body):
        if when is None:
            body()
        else:
            pl.when(when)(body)

    def taken(t):
        return takes if t else None

    def arrived(t, c, which, p, got):
        block = fr[t][c].at[4 * share(t)[which] + p]
        pltpu.make_async_copy(block, block, got).wait()

    def arrived_whole(t, c, which, got):
        def body():
            block = fr[t][c].at[pl.ds(4 * share(t)[which], 4)]
            pltpu.make_async_copy(block, block, got).wait()

        gated(taken(t), body)

    def greet():
        pl.semaphore_wait(barrier, 2 + gives.astype(jnp.int32))

    def gather(c):
        for p in range(NJ):
            src = pend_h.at[p, :, c * HW : (c + 1) * HW]
            dst = fr[0][c].at[4 * sub + p]
            send(src, dst, 0, recv_x.at[0, c, p], x_id)
        for p in range(NJ):
            src = pend_h.at[p, :, c * HW : (c + 1) * HW]
            dst = fr[0][c].at[4 * sub + p]
            send(src, dst, 0, recv_s.at[0, c], sib_id)

    def fwd_z(t, c, *ps):
        def body():
            for p in ps:
                got = recv_z.at[t - 1, c, p]
                arrived(t, c, 0, p, got)
                block = fr[t][c].at[4 * share(t)[0] + p]
                send(block, block, 1, recv_s.at[t, c], sib_id)
                send(block, block, 1, recv_x.at[t, c, p], x_id)

        gated(taken(t), body)

    def fwd_x(t, c, *ps):
        def body():
            for p in ps:
                arrived(t, c, 2, p, recv_x.at[t, c, p])
                block = fr[t][c].at[4 * share(t)[2] + p]
                send(block, block, min(t, 1), recv_xs.at[t, c], sib_id)

        gated(taken(t), body)

    def arr_s(t, c):
        arrived_whole(t, c, 1, recv_s.at[t, c])

    def arr_xs(t, c):
        arrived_whole(t, c, 3, recv_xs.at[t, c])

    def place(i, carry):
        own_links = [iidx[k, i] for k in range(NL)]
        for f in range(NF):
            at = jnp.int32(NL)
            for k in range(NL):
                at = jnp.where(own_links[k] == f, jnp.int32(k), at)
            pos[i * NF + f] = at
        return carry

    def places():
        for copy in ld_idx:
            copy.wait()
        lax.fori_loop(0, NI, place, 0)
        for i in range(NI):
            a[i, NL] = jnp.zeros((BL, BL), BF)

        @pl.when(slab == 0)
        def _():
            for t in range(1, NT):
                for c in range(2):
                    fr[t][c][...] = jnp.zeros((NF, BL, HW), BF)

    def a_wait(g):
        if g == 0:
            ld_inv.wait()
        ld_a[g].wait()

    def a_step(g):
        for i in range(4 * g, 4 * g + 4):
            for m in range(0, NL, 2):
                o = mm(inv[i], lanes([a[i, m], a[i, m + 1]]))
                o = (-o).astype(BF)
                a[i, m] = o[:, :BL]
                a[i, m + 1] = o[:, BL:]

    def b_wait():
        ld_finv.wait()
        ld_b.wait()

    def b_step():
        for j in range(NJ):
            for m in range(0, NK, 2):
                o = mm(finv[j], lanes([b[j, m], b[j, m + 1]]))
                o = (-o).astype(BF)
                b[j, m] = o[:, :BL]
                b[j, m + 1] = o[:, BL:]

    def c_step(*gs):
        for g in gs:
            for j in range(NJ):
                tiles = []
                for k in range(NK):
                    at = oidx[j, k]
                    tiles.append(
                        lanes(
                            [
                                a[at, pos[at * NF + 2 * g]],
                                a[at, pos[at * NF + 2 * g + 1]],
                            ]
                        )
                    )
                o = mm(lanes([b[j, k] for k in range(NK)]), rows(tiles)).astype(BF)
                cmat[2 * g, pl.ds(j * BL, BL)] = o[:, :BL]
                cmat[2 * g + 1, pl.ds(j * BL, BL)] = o[:, BL:]

    def p_step(t):
        ld_r[t].wait()
        for i in range(NI):
            o = mm(inv[i], rhs[t, i])
            if t < 2:
                p32[t, i] = o
            else:
                p2[i] = o
            if t:
                pbf[t - 1, i] = o.astype(BF)

    def front_left(j):
        return lanes([finv[j]] + [b[j, k] for k in range(NK)])

    def w_step(t):
        for j in range(NJ):
            right = rows(
                [front[j, :, t * CW : (t + 1) * CW]]
                + [pbf[t - 1, oidx[j, k]] for k in range(NK)]
            )
            o = mm(front_left(j), right)
            w[t][0, pl.ds(j * BL, BL)] = o[:, :HW]
            w[t][1, pl.ds(j * BL, BL)] = o[:, HW:]

    def acc2(t, c):
        arr_s(t, c)
        sh = share(t)
        w[t][c] = w[t][c] + dense(cmat, fr[t][c], sh[:2])

    def acc1(t, c):
        w[t][c] = w[t][c] + dense(cmat, fr[t][c], share(t)[2:3])

    def pass_on(t, c, *ps):
        def body():
            for p in ps:
                dst = fr[t + 1][c].at[4 * sub + p]
                got = recv_z.at[t, c, p]
                send(ysend.at[t, c, p], dst, 2, got, next_id)

        gated(gives, body)

    def y_step(t, c):
        arr_xs(t, c)
        sh = share(t)[3]
        right = fr[t][c][pl.ds(4 * sh, 4)].reshape(4 * BL, HW)
        for j in (0, 2):
            at = pl.ds(j * BL, 2 * BL)
            left = lanes([cmat[4 * sh + r, at] for r in range(4)])
            value = (w[t][c, at] + mm(left, right)).astype(BF).reshape(2, BL, HW)
            if t + 1 < NT:
                ysend[t, c, pl.ds(j, 2)] = value
                if j:
                    pass_on(t, c, *range(NJ))
            fro[j : j + 2, :, columns(t, c)] = value

    def s0_wait(c):
        own[c].wait()
        arr_s(0, c)
        arr_xs(0, c)

    def s0_step(c, *ids):
        for i in ids:
            base = p32[0, i, :, c * HW : (c + 1) * HW]
            o = base + interior(a, fr[0][c : c + 1], iidx, i)
            sol[i, :, columns(0, c)] = o.astype(BF)

    def y0_step(c):
        for j in range(NJ):
            right = rows(
                [front[j, :, columns(0, c)]]
                + [sol[oidx[j, k], :, columns(0, c)] for k in range(NK)]
            )
            value = mm(front_left(j), right).astype(BF)
            ysend[0, c, j] = value
            fro[j, :, columns(0, c)] = value
        pass_on(0, c, *range(NJ))

    def s_step(t, *ids):
        for i in ids:
            o = (p32[t, i] + interior(a, fr[t], iidx, i)).astype(BF)
            sol[i, :, t * CW : (t + 1) * CW] = o

    def s2_step():
        for i in range(NI):
            o = p2[i, :, :HW] + interior(a, fr[2][:1], iidx, i)
            sol[i, :, columns(2, 0)] = o.astype(BF)

    greet()
    gather(0)
    places()
    for g in range(4):
        a_wait(g)
        a_step(g)
    gather(1)
    late_loads()
    b_wait()
    b_step()
    p_step(0)
    fwd_x(0, 0, 0)
    c_step(0)
    fwd_x(0, 0, 1)
    c_step(1)
    fwd_x(0, 0, 2)
    ld_g.wait()
    fwd_x(0, 0, 3)
    c_step(2, 3)
    s0_wait(0)
    s0_step(0, *range(16))
    y0_step(0)
    fwd_x(0, 1, 0, 1, 2, 3)
    c_step(4, 5)
    s0_wait(1)
    s0_step(1, *range(16))
    y0_step(1)
    fwd_z(1, 0, 0)
    c_step(6)
    fwd_z(1, 0, 1)
    c_step(7)
    fwd_z(1, 0, 2)
    p_step(1)
    fwd_z(1, 0, 3)
    w_step(1)
    fwd_z(1, 1, 0)
    acc2(1, 0)
    fwd_x(1, 0, 0)
    fwd_z(1, 1, 1)
    fwd_x(1, 0, 1)
    fwd_x(1, 0, 2)
    fwd_z(1, 1, 2)
    fwd_x(1, 0, 3)
    fwd_z(1, 1, 3)
    acc1(1, 0)
    y_step(1, 0)
    fwd_x(1, 1, 0, 1)
    acc2(1, 1)
    fwd_x(1, 1, 2, 3)
    acc1(1, 1)
    y_step(1, 1)
    fwd_z(2, 0, 0)
    s_step(1, *range(0, 4))
    fwd_z(2, 0, 1)
    s_step(1, *range(4, 8))
    fwd_z(2, 0, 2)
    s_step(1, *range(8, 12))
    fwd_z(2, 0, 3)
    s_step(1, *range(12, 16))
    fwd_z(2, 1, 0)
    p_step(2)
    fwd_x(2, 0, 0)
    fwd_z(2, 1, 1)
    w_step(2)
    fwd_x(2, 0, 1)
    fwd_z(2, 1, 2)
    acc2(2, 0)
    fwd_x(2, 0, 2)
    fwd_z(2, 1, 3)
    fwd_x(2, 0, 3)
    acc1(2, 0)
    fwd_x(2, 1, 0)
    acc2(2, 1)
    fwd_x(2, 1, 1)
    y_step(2, 0)
    fwd_x(2, 1, 2, 3)
    acc1(2, 1)
    s2_step()
    arr_xs(2, 1)

    def finish():
        def gone(kind, ref):
            pltpu.make_async_copy(ref, ref, sent.at[kind]).wait()

        gone(0, rhs.at[:, pl.ds(0, 4)])
        gated(takes, lambda: gone(1, rhs.at[:, pl.ds(0, 8)]))
        gated(gives, lambda: gone(2, ysend))

    finish()


def last(iidx_h, most, fro01, f21, a, p2, cmat, w2, sol, fro, s, y, iidx, sem):
    moves = []

    def move(src, dst):
        copy = pltpu.make_async_copy(src, dst, sem.at[len(moves)])
        copy.start()
        moves.append(copy)
        return copy

    cut = NT * CW - HW
    links = move(iidx_h, iidx)
    move(most, sol.at[:, :, :cut])
    move(fro01.at[:, :, :cut], fro.at[:, :, :cut])
    sh = shares_of(source_of(lax.axis_index("slab"), lax.axis_index("sub")))
    value = w2[1] + dense(cmat, f21, sh[3:])
    y[...] = value.astype(BF).reshape(NJ, BL, HW)
    move(y, fro.at[:, :, cut:])
    links.wait()
    for first, count in ((0, 8), (8, 8)):
        for i in range(first, first + count):
            o = p2[i, :, HW:] + interior(a, (f21,), iidx, i)
            s[i] = o.astype(BF)
        at = pl.ds(first, count)
        move(s.at[at], sol.at[at, :, cut:])
    for copy in moves[1:]:
        copy.wait()


def solution(mesh):
    n_slab = mesh.shape["slab"]

    def shards(rhs, front, pend, iidx, a, inv, oidx, b, finv):
        vmem = pl.BlockSpec(memory_space=pltpu.VMEM)
        hbm = pl.BlockSpec(memory_space=pltpu.HBM)
        dma = pltpu.SemaphoreType.DMA
        half = pltpu.VMEM((NF, BL, HW), BF)
        def in_hbm(x):
            return pltpu.with_memory_space_constraint(x, pltpu.HBM)

        def in_vmem(x):
            return pltpu.with_memory_space_constraint(x, pltpu.VMEM)

        iidx = in_hbm(iidx.T)
        made = pl.pallas_call(
            lambda *refs: kernel(n_slab, *refs),
            name="substitution",
            out_shape=(
                pltpu.VMEM((NI, BL, NT * CW - HW), BF),
                pltpu.VMEM((NJ, BL, NT * CW), BF),
                half,
                pltpu.VMEM((NI, NL + 1, BL, BL), BF),
                pltpu.VMEM((NI, BL, CW), F32),
                pltpu.VMEM((NF, NJ * BL, BL), BF),
                pltpu.VMEM((2, NJ * BL, HW), F32),
            ),
            in_specs=[hbm] * 9,
            out_specs=(vmem,) * 7,
            scratch_shapes=[half] * 5
            + [
                pltpu.VMEM((NI, BL, BL), BF),
                pltpu.VMEM((NJ, NK, BL, BL), BF),
                pltpu.VMEM((NJ, BL, BL), BF),
                pltpu.VMEM((NT, NI, BL, CW), BF),
                pltpu.VMEM((NJ, BL, NT * CW), BF),
                pltpu.VMEM((2, NI, BL, CW), F32),
                pltpu.VMEM((2, NI, BL, CW), BF),
                pltpu.VMEM((2, NJ * BL, HW), F32),
                pltpu.VMEM((2, 2, NJ, BL, HW), BF),
                pltpu.SMEM((NL, NI), jnp.int32),
                pltpu.SMEM((NJ, NK), jnp.int32),
                pltpu.SMEM((NI * NF,), jnp.int32),
                dma((15,)),
                dma((3,)),
                dma((NT - 1, 2, NJ)),
                dma((NT, 2, NJ)),
                dma((NT, 2)),
                dma((NT, 2)),
            ],
            compiler_params=pltpu.CompilerParams(
                collective_id=0,
                has_side_effects=True,
                vmem_limit_bytes=30 * 1024 * 1024,
            ),
        )(
            iidx,
            *(
                in_hbm(x)
                for x in (
                    oidx,
                    rhs.reshape(NI, BL, NT * CW),
                    front.reshape(NJ, BL, NT * CW),
                    pend.reshape(NJ, BL, CW),
                    a,
                    inv,
                    b,
                    finv,
                )
            )
        )
        sol, fro = pl.pallas_call(
            last,
            name="last",
            out_shape=(
                pltpu.HBM((NI, BL, NT * CW), BF),
                pltpu.HBM((NJ, BL, NT * CW), BF),
            ),
            in_specs=[hbm] + [vmem] * 7,
            out_specs=(hbm, hbm),
            scratch_shapes=[
                pltpu.VMEM((NI, BL, HW), BF),
                pltpu.VMEM((NJ, BL, HW), BF),
                pltpu.SMEM((NL, NI), jnp.int32),
                dma((6,)),
            ],
            compiler_params=pltpu.CompilerParams(
                vmem_limit_bytes=30 * 1024 * 1024,
            ),
        )(iidx, *(in_vmem(x) for x in made))
        return sol.reshape(NI * BL, NT * CW), fro.reshape(NJ * BL, NT * CW)

    both = ("slab", "sub")
    two = P(both, None)
    return jax.shard_map(
        shards,
        mesh=mesh,
        in_specs=(
            two,
            two,
            two,
            two,
            P(both, None, None, None),
            P(both, None, None),
            two,
            P(both, None, None, None),
            P(both, None, None),
        ),
        out_specs=(two, two),
        check_vma=False,
    )
```

```python
import jax
import jax.numpy as jnp
from jax import lax
from jax.experimental import pallas as pl
from jax.experimental.pallas import tpu as pltpu
from jax.sharding import PartitionSpec as P

BF = jnp.bfloat16
F32 = jnp.float32
MESH = pl.DeviceIdType.MESH
BL = 128
NI = 16
NL = 6
NJ = 4
NK = 8
NF = 16
NT = 3
CW = 256
HW = 128


def lanes(parts):
    return jnp.concatenate(parts, axis=1)


def rows(parts):
    return jnp.concatenate(parts, axis=0)


def mm(a, b):
    return jnp.dot(a, b, preferred_element_type=F32)


def source_of(slab, sub):
    return (sub + 2 * (slab % 8 == 0).astype(jnp.int32)) % 4


def shares_of(base):
    one = base + 1 - 2 * (base % 2)
    return (base, one, (base + 2) % 4, (one + 2) % 4)


def columns(t, c):
    return slice(t * CW + c * HW, t * CW + (c + 1) * HW)


def dense(cmat, front_half, shares):
    left = lanes([cmat[4 * sh + r] for sh in shares for r in range(4)])
    right = rows([front_half[pl.ds(4 * sh, 4)].reshape(4 * BL, HW) for sh in shares])
    return mm(left, right)


def interior(a, halves, iidx, i):
    left = lanes([a[i, k] for k in range(NL)])
    right = rows([lanes([half[iidx[k, i]] for half in halves]) for k in range(NL)])
    return mm(left, right)


def kernel(
    n_slab,
    iidx_h,
    oidx_h,
    rhs_h,
    front_h,
    pend_h,
    a_h,
    inv_h,
    b_h,
    finv_h,
    sol,
    fro,
    f21,
    a,
    p2,
    cmat,
    w2,
    f00,
    f01,
    f10,
    f11,
    f20,
    inv,
    b,
    finv,
    rhs,
    front,
    p32,
    pbf,
    w1,
    ysend,
    iidx,
    oidx,
    pos,
    load_sem,
    sent,
    recv_z,
    recv_x,
    recv_s,
    recv_xs,
):
    fr = ((f00, f01), (f10, f11), (f20, f21))
    w = (None, w1, w2)
    slab = lax.axis_index("slab")
    sub = lax.axis_index("sub")
    sib = sub + 1 - 2 * (sub % 2)
    xp = (sub + 2) % 4
    to_sub = (sub + 2 * ((slab + 1) % 8 == 0).astype(jnp.int32)) % 4
    from_sub = source_of(slab, sub)
    gives = slab < n_slab - 1
    takes = slab > 0
    sib_id = (slab, sib)
    x_id = (slab, xp)
    next_id = ((slab + 1) % n_slab, to_sub)
    prev_id = ((slab + n_slab - 1) % n_slab, from_sub)

    barrier = pltpu.get_barrier_semaphore()
    for peer in (sib_id, x_id):
        pl.semaphore_signal(barrier, inc=1, device_id=peer, device_id_type=MESH)

    @pl.when(takes)
    def _():
        pl.semaphore_signal(barrier, inc=1, device_id=prev_id, device_id_type=MESH)

    def share(t):
        return shares_of(sub if t == 0 else from_sub)

    loads = []

    def load(src, dst):
        copy = pltpu.make_async_copy(src, dst, load_sem.at[len(loads)])
        copy.start()
        loads.append(copy)
        return copy

    ld_idx = [load(iidx_h, iidx), load(oidx_h, oidx)]
    ld_inv = load(inv_h, inv)
    ld_a = [
        load(a_h.at[pl.ds(4 * g, 4)], a.at[pl.ds(4 * g, 4), pl.ds(0, NL)])
        for g in range(4)
    ]
    ld_finv = load(finv_h, finv)
    ld_b = load(b_h, b)
    ld_r = [load(rhs_h.at[:, :, 0:CW], rhs.at[0])]
    own = [
        load(
            pend_h.at[:, :, c * HW : (c + 1) * HW],
            fr[0][c].at[pl.ds(4 * sub, 4)],
        )
        for c in range(2)
    ]
    ld_g = load(front_h, front)

    def late_loads():
        for t in range(1, NT):
            ld_r.append(load(rhs_h.at[:, :, t * CW : (t + 1) * CW], rhs.at[t]))

    def send(src, dst, kind, got, peer):
        pltpu.make_async_remote_copy(
            src_ref=src,
            dst_ref=dst,
            send_sem=sent.at[kind],
            recv_sem=got,
            device_id=peer,
            device_id_type=MESH,
        ).start()

    def gated(when, body):
        if when is None:
            body()
        else:
            pl.when(when)(body)

    def taken(t):
        return takes if t else None

    def arrived(t, c, which, p, got):
        block = fr[t][c].at[4 * share(t)[which] + p]
        pltpu.make_async_copy(block, block, got).wait()

    def arrived_whole(t, c, which, got):
        def body():
            block = fr[t][c].at[pl.ds(4 * share(t)[which], 4)]
            pltpu.make_async_copy(block, block, got).wait()

        gated(taken(t), body)

    def greet():
        pl.semaphore_wait(barrier, 2 + gives.astype(jnp.int32))

    def gather(c):
        for p in range(NJ):
            src = pend_h.at[p, :, c * HW : (c + 1) * HW]
            dst = fr[0][c].at[4 * sub + p]
            send(src, dst, 0, recv_x.at[0, c, p], x_id)
        for p in range(NJ):
            src = pend_h.at[p, :, c * HW : (c + 1) * HW]
            dst = fr[0][c].at[4 * sub + p]
            send(src, dst, 0, recv_s.at[0, c], sib_id)

    def fwd_z(t, c, *ps):
        def body():
            for p in ps:
                got = recv_z.at[t - 1, c, p]
                arrived(t, c, 0, p, got)
                block = fr[t][c].at[4 * share(t)[0] + p]
                send(block, block, 1, recv_s.at[t, c], sib_id)
                send(block, block, 1, recv_x.at[t, c, p], x_id)

        gated(taken(t), body)

    def fwd_x(t, c, *ps):
        def body():
            for p in ps:
                arrived(t, c, 2, p, recv_x.at[t, c, p])
                block = fr[t][c].at[4 * share(t)[2] + p]
                send(block, block, min(t, 1), recv_xs.at[t, c], sib_id)

        gated(taken(t), body)

    def arr_s(t, c):
        arrived_whole(t, c, 1, recv_s.at[t, c])

    def arr_xs(t, c):
        arrived_whole(t, c, 3, recv_xs.at[t, c])

    def place(i, carry):
        own_links = [iidx[k, i] for k in range(NL)]
        for f in range(NF):
            at = jnp.int32(NL)
            for k in range(NL):
                at = jnp.where(own_links[k] == f, jnp.int32(k), at)
            pos[i * NF + f] = at
        return carry

    def places():
        for copy in ld_idx:
            copy.wait()
        lax.fori_loop(0, NI, place, 0)
        for i in range(NI):
            a[i, NL] = jnp.zeros((BL, BL), BF)

        @pl.when(slab == 0)
        def _():
            for t in range(1, NT):
                for c in range(2):
                    fr[t][c][...] = jnp.zeros((NF, BL, HW), BF)

    def a_wait(g):
        if g == 0:
            ld_inv.wait()
        ld_a[g].wait()

    def a_step(g):
        for i in range(4 * g, 4 * g + 4):
            for m in range(0, NL, 2):
                o = mm(inv[i], lanes([a[i, m], a[i, m + 1]]))
                o = (-o).astype(BF)
                a[i, m] = o[:, :BL]
                a[i, m + 1] = o[:, BL:]

    def b_wait():
        ld_finv.wait()
        ld_b.wait()

    def b_step():
        for j in range(NJ):
            for m in range(0, NK, 2):
                o = mm(finv[j], lanes([b[j, m], b[j, m + 1]]))
                o = (-o).astype(BF)
                b[j, m] = o[:, :BL]
                b[j, m + 1] = o[:, BL:]

    def c_step(*gs):
        for g in gs:
            for j in range(NJ):
                tiles = []
                for k in range(NK):
                    at = oidx[j, k]
                    tiles.append(
                        lanes(
                            [
                                a[at, pos[at * NF + 2 * g]],
                                a[at, pos[at * NF + 2 * g + 1]],
                            ]
                        )
                    )
                o = mm(lanes([b[j, k] for k in range(NK)]), rows(tiles)).astype(BF)
                cmat[2 * g, pl.ds(j * BL, BL)] = o[:, :BL]
                cmat[2 * g + 1, pl.ds(j * BL, BL)] = o[:, BL:]

    def p_step(t):
        ld_r[t].wait()
        for i in range(NI):
            o = mm(inv[i], rhs[t, i])
            if t < 2:
                p32[t, i] = o
            else:
                p2[i] = o
            if t:
                pbf[t - 1, i] = o.astype(BF)

    def front_left(j):
        return lanes([finv[j]] + [b[j, k] for k in range(NK)])

    def w_step(t):
        for j in range(NJ):
            right = rows(
                [front[j, :, t * CW : (t + 1) * CW]]
                + [pbf[t - 1, oidx[j, k]] for k in range(NK)]
            )
            o = mm(front_left(j), right)
            w[t][0, pl.ds(j * BL, BL)] = o[:, :HW]
            w[t][1, pl.ds(j * BL, BL)] = o[:, HW:]

    def acc2(t, c):
        arr_s(t, c)
        sh = share(t)
        w[t][c] = w[t][c] + dense(cmat, fr[t][c], sh[:2])

    def acc1(t, c):
        w[t][c] = w[t][c] + dense(cmat, fr[t][c], share(t)[2:3])

    def pass_on(t, c, *ps):
        def body():
            for p in ps:
                dst = fr[t + 1][c].at[4 * sub + p]
                got = recv_z.at[t, c, p]
                send(ysend.at[t, c, p], dst, 2, got, next_id)

        gated(gives, body)

    def y_step(t, c):
        arr_xs(t, c)
        sh = share(t)[3]
        right = fr[t][c][pl.ds(4 * sh, 4)].reshape(4 * BL, HW)
        for j in (0, 2):
            at = pl.ds(j * BL, 2 * BL)
            left = lanes([cmat[4 * sh + r, at] for r in range(4)])
            value = (w[t][c, at] + mm(left, right)).astype(BF).reshape(2, BL, HW)
            if t + 1 < NT:
                ysend[t, c, pl.ds(j, 2)] = value
                if j:
                    pass_on(t, c, *range(NJ))
            fro[j : j + 2, :, columns(t, c)] = value

    def s0_wait(c):
        own[c].wait()
        arr_s(0, c)
        arr_xs(0, c)

    def s0_step(c, *ids):
        for i in ids:
            base = p32[0, i, :, c * HW : (c + 1) * HW]
            o = base + interior(a, fr[0][c : c + 1], iidx, i)
            sol[i, :, columns(0, c)] = o.astype(BF)

    def y0_step(c):
        for j in range(NJ):
            right = rows(
                [front[j, :, columns(0, c)]]
                + [sol[oidx[j, k], :, columns(0, c)] for k in range(NK)]
            )
            value = mm(front_left(j), right).astype(BF)
            ysend[0, c, j] = value
            fro[j, :, columns(0, c)] = value
        pass_on(0, c, *range(NJ))

    def s_step(t, *ids):
        for i in ids:
            o = (p32[t, i] + interior(a, fr[t], iidx, i)).astype(BF)
            sol[i, :, t * CW : (t + 1) * CW] = o

    def s2_step():
        for i in range(NI):
            o = p2[i, :, :HW] + interior(a, fr[2][:1], iidx, i)
            sol[i, :, columns(2, 0)] = o.astype(BF)

    greet()
    gather(0)
    places()
    for g in range(4):
        a_wait(g)
        a_step(g)
    gather(1)
    late_loads()
    b_wait()
    b_step()
    p_step(0)
    fwd_x(0, 0, 0)
    c_step(0)
    fwd_x(0, 0, 1)
    c_step(1)
    fwd_x(0, 0, 2)
    ld_g.wait()
    fwd_x(0, 0, 3)
    c_step(2, 3)
    s0_wait(0)
    s0_step(0, *range(16))
    y0_step(0)
    fwd_x(0, 1, 0, 1, 2, 3)
    c_step(4, 5)
    s0_wait(1)
    s0_step(1, *range(16))
    y0_step(1)
    fwd_z(1, 0, 0)
    c_step(6)
    fwd_z(1, 0, 1)
    c_step(7)
    fwd_z(1, 0, 2)
    p_step(1)
    fwd_z(1, 0, 3)
    w_step(1)
    fwd_z(1, 1, 0)
    acc2(1, 0)
    fwd_x(1, 0, 0)
    fwd_z(1, 1, 1)
    fwd_x(1, 0, 1)
    fwd_x(1, 0, 2)
    fwd_z(1, 1, 2)
    fwd_x(1, 0, 3)
    fwd_z(1, 1, 3)
    acc1(1, 0)
    y_step(1, 0)
    fwd_x(1, 1, 0, 1)
    acc2(1, 1)
    fwd_x(1, 1, 2, 3)
    acc1(1, 1)
    y_step(1, 1)
    fwd_z(2, 0, 0)
    s_step(1, *range(0, 4))
    fwd_z(2, 0, 1)
    s_step(1, *range(4, 8))
    fwd_z(2, 0, 2)
    s_step(1, *range(8, 12))
    fwd_z(2, 0, 3)
    s_step(1, *range(12, 16))
    fwd_z(2, 1, 0)
    p_step(2)
    fwd_x(2, 0, 0)
    fwd_z(2, 1, 1)
    w_step(2)
    fwd_x(2, 0, 1)
    fwd_z(2, 1, 2)
    acc2(2, 0)
    fwd_x(2, 0, 2)
    fwd_z(2, 1, 3)
    fwd_x(2, 0, 3)
    acc1(2, 0)
    fwd_x(2, 1, 0)
    acc2(2, 1)
    fwd_x(2, 1, 1)
    y_step(2, 0)
    fwd_x(2, 1, 2, 3)
    acc1(2, 1)
    s2_step()
    arr_xs(2, 1)

    def finish():
        def gone(kind, ref):
            pltpu.make_async_copy(ref, ref, sent.at[kind]).wait()

        gone(0, rhs.at[:, pl.ds(0, 4)])
        gated(takes, lambda: gone(1, rhs.at[:, pl.ds(0, 8)]))
        gated(gives, lambda: gone(2, ysend))

    finish()


def last(iidx_h, most, fro01, f21, a, p2, cmat, w2, sol, fro, s, y, iidx, sem):
    moves = []

    def move(src, dst):
        copy = pltpu.make_async_copy(src, dst, sem.at[len(moves)])
        copy.start()
        moves.append(copy)
        return copy

    cut = NT * CW - HW
    links = move(iidx_h, iidx)
    move(most, sol.at[:, :, :cut])
    move(fro01.at[:, :, :cut], fro.at[:, :, :cut])
    sh = shares_of(source_of(lax.axis_index("slab"), lax.axis_index("sub")))
    value = w2[1] + dense(cmat, f21, sh[3:])
    y[...] = value.astype(BF).reshape(NJ, BL, HW)
    move(y, fro.at[:, :, cut:])
    links.wait()
    for first, count in ((0, 12), (12, 4)):
        for i in range(first, first + count):
            o = p2[i, :, HW:] + interior(a, (f21,), iidx, i)
            s[i] = o.astype(BF)
        at = pl.ds(first, count)
        move(s.at[at], sol.at[at, :, cut:])
    for copy in moves[1:]:
        copy.wait()


def solution(mesh):
    n_slab = mesh.shape["slab"]

    def shards(rhs, front, pend, iidx, a, inv, oidx, b, finv):
        vmem = pl.BlockSpec(memory_space=pltpu.VMEM)
        hbm = pl.BlockSpec(memory_space=pltpu.HBM)
        dma = pltpu.SemaphoreType.DMA
        half = pltpu.VMEM((NF, BL, HW), BF)
        def in_hbm(x):
            return pltpu.with_memory_space_constraint(x, pltpu.HBM)

        def in_vmem(x):
            return pltpu.with_memory_space_constraint(x, pltpu.VMEM)

        iidx = in_hbm(iidx.T)
        made = pl.pallas_call(
            lambda *refs: kernel(n_slab, *refs),
            name="substitution",
            out_shape=(
                pltpu.VMEM((NI, BL, NT * CW - HW), BF),
                pltpu.VMEM((NJ, BL, NT * CW), BF),
                half,
                pltpu.VMEM((NI, NL + 1, BL, BL), BF),
                pltpu.VMEM((NI, BL, CW), F32),
                pltpu.VMEM((NF, NJ * BL, BL), BF),
                pltpu.VMEM((2, NJ * BL, HW), F32),
            ),
            in_specs=[hbm] * 9,
            out_specs=(vmem,) * 7,
            scratch_shapes=[half] * 5
            + [
                pltpu.VMEM((NI, BL, BL), BF),
                pltpu.VMEM((NJ, NK, BL, BL), BF),
                pltpu.VMEM((NJ, BL, BL), BF),
                pltpu.VMEM((NT, NI, BL, CW), BF),
                pltpu.VMEM((NJ, BL, NT * CW), BF),
                pltpu.VMEM((2, NI, BL, CW), F32),
                pltpu.VMEM((2, NI, BL, CW), BF),
                pltpu.VMEM((2, NJ * BL, HW), F32),
                pltpu.VMEM((2, 2, NJ, BL, HW), BF),
                pltpu.SMEM((NL, NI), jnp.int32),
                pltpu.SMEM((NJ, NK), jnp.int32),
                pltpu.SMEM((NI * NF,), jnp.int32),
                dma((15,)),
                dma((3,)),
                dma((NT - 1, 2, NJ)),
                dma((NT, 2, NJ)),
                dma((NT, 2)),
                dma((NT, 2)),
            ],
            compiler_params=pltpu.CompilerParams(
                collective_id=0,
                has_side_effects=True,
                vmem_limit_bytes=30 * 1024 * 1024,
            ),
        )(
            iidx,
            *(
                in_hbm(x)
                for x in (
                    oidx,
                    rhs.reshape(NI, BL, NT * CW),
                    front.reshape(NJ, BL, NT * CW),
                    pend.reshape(NJ, BL, CW),
                    a,
                    inv,
                    b,
                    finv,
                )
            )
        )
        sol, fro = pl.pallas_call(
            last,
            name="last",
            out_shape=(
                pltpu.HBM((NI, BL, NT * CW), BF),
                pltpu.HBM((NJ, BL, NT * CW), BF),
            ),
            in_specs=[hbm] + [vmem] * 7,
            out_specs=(hbm, hbm),
            scratch_shapes=[
                pltpu.VMEM((NI, BL, HW), BF),
                pltpu.VMEM((NJ, BL, HW), BF),
                pltpu.SMEM((NL, NI), jnp.int32),
                dma((6,)),
            ],
            compiler_params=pltpu.CompilerParams(
                vmem_limit_bytes=30 * 1024 * 1024,
            ),
        )(iidx, *(in_vmem(x) for x in made))
        return sol.reshape(NI * BL, NT * CW), fro.reshape(NJ * BL, NT * CW)

    both = ("slab", "sub")
    two = P(both, None)
    return jax.shard_map(
        shards,
        mesh=mesh,
        in_specs=(
            two,
            two,
            two,
            two,
            P(both, None, None, None),
            P(both, None, None),
            two,
            P(both, None, None, None),
            P(both, None, None),
        ),
        out_specs=(two, two),
        check_vma=False,
    )
```
